1024 devices in a mesh: section: 64 (over y, z_lo, core), dp: 16 (over x, z_hi).
Axes of the slice: x: 4, y: 4, z: 32 (z_hi: 4, z_lo: 8; z = z_hi * 8 + z_lo), core: 2. Of those that a mesh axis runs over, the one named last changes fastest.
Arguments:
- signal: bfloat16 [16384, 4096], P('section', 'dp'), may hold values from -6 to 6
- mixing: bfloat16 [3, 4096, 4096], P(None, 'dp'), may hold values from -0.046875 to 0.046875
- taps: float32 [3, 4, 4096], P(None, None, 'dp'), may hold values from -3 to 3
- offsets: int32 [3, 4], replicated, may hold values from 0 to 63, as said below
Outputs:
- layer_outputs: bfloat16 [3, 16384, 4096], P(None, 'section', 'dp')
The draws below stay inside these ranges and needn't reach their ends.
Inputs may be any that keep to these rules, and one draw needn't show every extreme that they name: Each layer's 4 offsets are distinct and include 0 and 63.
All inputs are finite; a program needn't handle non-finite values.
Results may differ from the reference program's by a relative error of at most 0.015.
Values may be sent and summed in bfloat16 or wider, within the bound.
No kernel may reach another device: no remote copies, remote signals or barrier semaphores. Data moves between devices by JAX's collectives and lax.ppermute only.
A program may use at most 32 MiB of HBM per device.

```python
import jax
import jax.numpy as jnp
from jax import lax

C = 4096
TAPS = 4
REACH = 64
LAYERS = 3
SEQ = 16384
N_DP = 16


def draw_offsets(key, part):

    def one_layer(layer):
        layer_key = jax.random.fold_in(jax.random.fold_in(key, 17), layer)
        middle = jax.random.permutation(layer_key, REACH - 2) + 1
        chosen = jnp.concatenate([jnp.array([0, REACH - 1], jnp.int32), middle[:TAPS - 2].astype(jnp.int32)])
        order_key = jax.random.fold_in(layer_key, 5)
        return jax.random.permutation(order_key, chosen).astype(jnp.int32)
    return jax.vmap(one_layer)(jnp.arange(LAYERS, dtype=jnp.int32))


def raised(values, stream_key, source, target, shards_of, factor):
    def block_of(dim):
        return (jnp.arange(values.shape[dim]) // (values.shape[dim] // shards_of)).reshape((-1,) + (1,) * (values.ndim - 1 - dim))

    first = jax.random.permutation(stream_key, shards_of)[block_of(target)]
    second = (block_of(target) + shards_of // 2) % shards_of
    return jnp.where((block_of(source) == first) | (block_of(source) == second), factor * values, values)


def steps_of(stream_key, dims, pieces, low, top_value):
    gain, own = 1.0, jax.random.fold_in(stream_key, 6)
    for axis_at, shards_of in pieces:
        draws = jnp.exp(jax.random.uniform(jax.random.fold_in(own, axis_at), (shards_of,), jnp.float32, low / len(pieces), top_value / len(pieces)))
        gain = gain * jnp.repeat(draws, dims[axis_at] // shards_of).reshape([-1 if axis == axis_at else 1 for axis in range(len(dims))])
    return gain


def centred(key, shape, spread, most, pieces=(), held_as=jnp.bfloat16):
    values = jax.random.normal(key, shape, jnp.float32) * spread
    if len(pieces) > 0:
        values = steps_of(key, shape, pieces, -0.22, 0.18) * values
    return jnp.clip(values, min=-most, max=most).astype(held_as)


def bell_draw_with(stream_key, extent, deviation, reach, shards, heavy, kind=jnp.bfloat16):
    values = deviation * jax.random.normal(stream_key, extent, jnp.float32)
    if shards:
        values = values * steps_of(stream_key, extent, shards, -0.22, 0.18)
    return jnp.clip(raised(values, jax.random.fold_in(stream_key, 3), *heavy), -reach, reach).astype(kind)


def setup_inputs(seed: int = 0) -> dict:
    splits = jax.random.split(jax.random.key(seed), 5)
    return {
        "signal": centred(splits[0], (SEQ, C), 1.0, 6.0, ((0, 64), (1, 16))),
        "mixing": bell_draw_with(splits[1], (LAYERS, C, C), (8 * C) ** -0.5, 0.046875, ((1, 16),), (1, 2, 16, 2.0)),
        "taps": centred(splits[2], (LAYERS, TAPS, C), 0.35, 3.0, ((2, 16),), jnp.float32),
        "offsets": draw_offsets(jax.random.fold_in(splits[4], 71), 0),
    }


def one_layer(hidden, params):
    weights, coeffs, shifts = params
    values = hidden.astype(jnp.float32)
    normed = values * lax.rsqrt(lax.optimization_barrier(jnp.mean(values * values, axis=-1, keepdims=True)) + 1e-06)
    stored = lax.optimization_barrier(normed.astype(jnp.bfloat16)).astype(jnp.float32)
    padded = jnp.concatenate([jnp.zeros((REACH - 1, C), jnp.float32), stored], axis=0)
    conv = jnp.zeros((SEQ, C), jnp.float32)
    for k in range(TAPS):
        start = (REACH - 1 - shifts[k]).astype(jnp.int32)
        window = lax.dynamic_slice_in_dim(padded, start, SEQ, 0)
        conv = conv + coeffs[k] * window
    gated = (conv * jax.nn.silu(normed)).astype(jnp.bfloat16)
    share = C // N_DP
    mixed = jnp.zeros((SEQ, C), jnp.float32)
    for part_index in range(N_DP):
        rows_in = gated[:, part_index * share:(part_index + 1) * share]
        rows_w = weights[part_index * share:(part_index + 1) * share, :]
        partial_term = jnp.dot(rows_in, rows_w, preferred_element_type=jnp.float32)
        partial_term = lax.optimization_barrier(partial_term.astype(jnp.bfloat16)).astype(jnp.float32)
        mixed = mixed + partial_term
    result = (values + mixed).astype(jnp.bfloat16)
    return (result, result)

def reference(signal, mixing, taps, offsets):
    final, outputs = lax.scan(one_layer, signal, (mixing, taps, offsets))
    return outputs
```

```python
import jax
import jax.numpy as jnp
from jax import lax
from jax.sharding import Mesh, PartitionSpec as P

C = 4096
REACH = 64
SECTION = ("y", "zl", "c")


def tiled_weights(mixing):
    layers, depth, width = mixing.shape
    n_x, n_zh = lax.axis_size("x"), lax.axis_size("zh")
    n_row = lax.axis_size("zl") * lax.axis_size("c")
    rows, columns = depth // n_row, width // n_x
    row_at = (lax.axis_index("zl") * lax.axis_size("c") + lax.axis_index("c")) * rows
    piece = lax.dynamic_slice(mixing, (0, row_at, lax.axis_index("y") * columns), (layers, rows, columns))
    piece = piece.reshape(layers, rows, n_zh, columns // n_zh)
    piece = lax.all_to_all(piece, "zh", split_axis=2, concat_axis=1)
    piece = lax.all_gather(piece, ("zl", "c"), axis=2, tiled=True)
    piece = piece.reshape(layers, n_zh * depth, columns // n_zh)
    return lax.all_gather(piece, "y", axis=0)


def body(signal, mixing, taps, offsets):
    row_count, channel_count = signal.shape
    n_section = lax.axis_size(SECTION)
    forward = [(source, source + 1) for source in range(n_section - 1)]
    tiles = tiled_weights(mixing)
    coeffs_all = lax.all_gather(taps, "zh", axis=2, tiled=True)
    hidden = signal
    results = []
    for layer in range(mixing.shape[0]):
        wide = lax.all_gather(hidden, "zh", axis=1, tiled=True)
        before = lax.ppermute(wide[row_count - REACH :], SECTION, forward)
        values = jnp.concatenate([before, wide], axis=0).astype(jnp.float32)
        squares = lax.psum(jnp.sum(values * values, axis=-1), "x")
        normed = values * lax.rsqrt(squares / C + 1e-06)[:, None]
        stored = normed.astype(jnp.bfloat16)
        conv = jnp.zeros((row_count, values.shape[1]), jnp.float32)
        for k in range(taps.shape[1]):
            window = lax.dynamic_slice_in_dim(stored, REACH - offsets[layer, k], row_count, 0)
            conv = conv + coeffs_all[layer, k] * window.astype(jnp.float32)
        gated = (conv * jax.nn.silu(normed[REACH:])).astype(jnp.bfloat16)
        partial = jnp.einsum("tk,xkn->xtn", gated, tiles[:, layer], preferred_element_type=jnp.float32)
        terms = lax.all_to_all(partial.astype(jnp.bfloat16), "x", split_axis=0, concat_axis=0)
        mixed = jnp.sum(terms.astype(jnp.float32), axis=0)
        hidden = (hidden.astype(jnp.float32) + mixed).astype(jnp.bfloat16)
        results.append(hidden)
    return jnp.stack(results)


def solution(mesh):
    fine = Mesh(mesh.devices.reshape(4, 8, 2, 4, 4), ("y", "zl", "c", "x", "zh"))
    dp = ("x", "zh")
    in_specs = (P(SECTION, dp), P(None, dp, None), P(None, None, dp), P())
    out_specs = P(None, SECTION, dp)
    return jax.shard_map(body, mesh=fine, in_specs=in_specs, out_specs=out_specs, check_vma=False)
```

```python
import jax
import jax.numpy as jnp
from jax import lax
from jax.sharding import Mesh, PartitionSpec as P

C = 4096
REACH = 64
SECTION = ("y", "zl", "c")


def rotated(value, axis, steps):
    count = lax.axis_size(axis)
    return lax.ppermute(value, axis, [(source, (source + steps) % count) for source in range(count)])


def crossed_weights(mixing):
    layers, depth, width = mixing.shape
    n_y, n_c, n_zh = lax.axis_size("y"), lax.axis_size("c"), lax.axis_size("zh")
    y, c = lax.axis_index("y"), lax.axis_index("c")
    columns = width // n_y
    rows = depth // n_c
    first = lax.dynamic_slice(mixing, (0, c * rows, y * columns), (1, rows, columns))
    first = first.reshape(rows, n_zh, columns // n_zh).transpose(1, 0, 2)
    few = depth // (lax.axis_size("zl") * n_c)
    rest = lax.dynamic_slice(
        mixing, (1, (lax.axis_index("zl") * n_c + c) * few, y * columns), (layers - 1, few, columns)
    )
    rest = rest.reshape(layers - 1, few, n_zh, columns // n_zh).transpose(2, 0, 1, 3)
    rest = rest.reshape(n_zh, (layers - 1) * few, columns // n_zh)
    got = lax.all_to_all(jnp.concatenate([first, rest], axis=1), "zh", split_axis=0, concat_axis=0)
    return got[:, :rows], got[:, rows:]


def later_tiles(rest, layers):
    n_zh, rows, columns = rest.shape
    few = rows // layers
    n_y = lax.axis_size("y")
    n_row = lax.axis_size("zl") * lax.axis_size("c")
    gathered = lax.all_gather(rest, SECTION, axis=0)
    gathered = gathered.reshape(n_y, n_row, n_zh, layers, few, columns).transpose(3, 0, 2, 1, 4, 5)
    return gathered.reshape(layers, n_y, n_zh * n_row * few, columns)


def body(signal, mixing, taps, offsets):
    row_count, channel_count = signal.shape
    layers, n_taps = taps.shape[:2]
    n_section = lax.axis_size(SECTION)
    n_y = lax.axis_size("y")
    forward = [(source, source + 1) for source in range(n_section - 1)]
    first, rest = crossed_weights(mixing)
    signal, first, rest = lax.optimization_barrier((signal, first, rest))
    later = later_tiles(rest, layers - 1)
    own = lax.all_gather(first, "c", axis=1, tiled=True).reshape(-1, channel_count)
    turned = jnp.stack([own] + [rotated(own, "y", k) for k in range(1, n_y)])
    high = lax.reduce_precision(taps, 8, 7)
    low = (taps - high).astype(jnp.bfloat16)
    tap_rows = jnp.concatenate(
        [high.astype(jnp.bfloat16).reshape(-1, channel_count), low.reshape(-1, channel_count)], axis=0
    )
    n_tap_rows = layers * n_taps
    tap_rows = jnp.pad(tap_rows, ((0, -2 * n_tap_rows % 16), (0, 0)))
    hidden = signal
    results = []
    for layer in range(layers):
        if layer == 0:
            wide = lax.all_gather(jnp.concatenate([hidden, tap_rows], axis=0), "zh", axis=1, tiled=True)
            coeffs = wide[row_count : row_count + 2 * n_tap_rows].astype(jnp.float32)
            coeffs = (coeffs[:n_tap_rows] + coeffs[n_tap_rows:]).reshape(layers, n_taps, -1)
            wide = wide[:row_count]
        else:
            wide = lax.all_gather(hidden, "zh", axis=1, tiled=True)
        before = lax.ppermute(wide[row_count - REACH :], SECTION, forward)
        values = jnp.concatenate([before, wide], axis=0).astype(jnp.float32)
        squares = lax.psum(jnp.sum(values * values, axis=-1), "x")
        normed = values * lax.rsqrt(squares / C + 1e-06)[:, None]
        stored = normed.astype(jnp.bfloat16)
        conv = jnp.zeros((row_count, values.shape[1]), jnp.float32)
        for k in range(n_taps):
            window = lax.dynamic_slice_in_dim(stored, REACH - offsets[layer, k], row_count, 0)
            conv = conv + coeffs[layer, k] * window.astype(jnp.float32)
        gated = (conv * jax.nn.silu(normed[REACH:])).astype(jnp.bfloat16)
        tile = turned if layer == 0 else later[layer - 1]
        partial = jnp.einsum("tk,xkn->xtn", gated, tile, preferred_element_type=jnp.float32).astype(jnp.bfloat16)
        if layer == 0:
            partial = partial[(lax.axis_index("y") - jnp.arange(n_y)) % n_y]
        terms = lax.all_to_all(partial, "x", split_axis=0, concat_axis=0)
        mixed = jnp.sum(terms.astype(jnp.float32), axis=0)
        hidden = (hidden.astype(jnp.float32) + mixed).astype(jnp.bfloat16)
        results.append(hidden)
    return jnp.stack(results)


def solution(mesh):
    fine = Mesh(mesh.devices.reshape(4, 8, 2, 4, 4), ("y", "zl", "c", "x", "zh"))
    dp = ("x", "zh")
    in_specs = (P(SECTION, dp), P(None, dp, None), P(None, None, dp), P())
    out_specs = P(None, SECTION, dp)
    return jax.shard_map(body, mesh=fine, in_specs=in_specs, out_specs=out_specs, check_vma=False)
```

```python
import jax
import jax.numpy as jnp
from jax import lax
from jax.sharding import Mesh, PartitionSpec as P

REACH = 64
SECTION = ("y", "zl", "c")
TURNED = ("y", "zl", "zh")
PLACE = ("zl", "c", "zh")


def turn_pairs(n_y, n_zl, n_zh):
    pairs = []
    for y in range(n_y):
        for zl in range(n_zl):
            for zh in range(n_zh):
                q, r = divmod(zl, 2)
                source = (y * n_zl + zl) * n_zh + zh
                target = (zh * n_zl + 2 * y + r) * n_zh + q
                pairs.append((source, target))
    return pairs


def halo_pairs(n_y, n_zl, n_c, n_zh):
    places = []
    for y in range(n_y):
        for zl in range(n_zl):
            for c in range(n_c):
                q, r = divmod(zl, 2)
                places.append(((2 * y + r) * n_c + c) * n_zh + q)
    return list(zip(places[:-1], places[1:]))


def crossed(value, axis, bit):
    return lax.ppermute(value, axis, [(i, i ^ bit) for i in range(lax.axis_size(axis))])


def after(value, *others):
    return lax.optimization_barrier((value, *others))[0]


def body(signal, mixing, taps, offsets):
    row_count, width = signal.shape
    layers, n_taps = taps.shape[:2]
    n_x, n_y, n_zl, n_c, n_zh = (lax.axis_size(a) for a in ("x", "y", "zl", "c", "zh"))
    y, zl, c = lax.axis_index("y"), lax.axis_index("zl"), lax.axis_index("c")
    total_channels = n_x * n_zh * width
    there = turn_pairs(n_y, n_zl, n_zh)
    back = [(target, source) for source, target in there]
    forward = halo_pairs(n_y, n_zl, n_c, n_zh)

    hidden = lax.ppermute(signal, TURNED, there)

    low_bits = zl % n_x
    half = width // n_c
    share = lax.dynamic_slice(mixing, (0, c * half, (low_bits * n_y + y) * width), (layers, half, width))
    high = lax.reduce_precision(taps, 8, 7)
    low = (taps - high).astype(jnp.bfloat16)
    n_tap_rows = layers * n_taps
    sent = jnp.concatenate(
        [
            share.reshape(layers * half, width),
            high.astype(jnp.bfloat16).reshape(n_tap_rows, width),
            low.reshape(n_tap_rows, width),
            jnp.zeros((-2 * n_tap_rows % 16, width), jnp.bfloat16),
        ],
        axis=0,
    )
    got = lax.all_gather(sent, "zh", axis=0)
    hidden, got = lax.optimization_barrier((hidden, got))
    coeffs = got[:, layers * half :].astype(jnp.float32)
    coeffs = coeffs[:, :n_tap_rows] + coeffs[:, n_tap_rows : 2 * n_tap_rows]
    coeffs = coeffs.transpose(1, 0, 2).reshape(layers, n_taps, n_zh * width)
    shares = got[:, : layers * half].reshape(n_zh, layers, half, width).transpose(1, 0, 2, 3)
    first = shares[:1].reshape(1, 1, n_zh * half, width)
    rest = shares[1:].reshape(1, layers - 1, n_zh * half, width)

    first = jnp.concatenate([first, crossed(first, "zl", 2)], axis=0)
    order = jnp.array([0, 2, 1, 3])
    entry_of = order[jnp.arange(n_x) ^ low_bits]
    results = []
    own = other = None
    for layer in range(layers):
        if layer == layers - 1:
            earlier = lax.ppermute(jnp.stack(results), TURNED, back)
        wide = lax.all_gather(hidden, "y", axis=1, tiled=True)
        if layer == 0:
            wide, first = lax.optimization_barrier((wide, first))
            first = jnp.concatenate([first, crossed(first, "zl", 1)], axis=0)
        else:
            own = rest[:, layer - 1]
            other = crossed(after(own, wide), "c", 1)
        before = lax.ppermute(wide[row_count - REACH :], PLACE, forward)
        values = jnp.concatenate([before, wide], axis=0).astype(jnp.float32)
        squares = lax.psum(jnp.sum(values * values, axis=-1), "x")
        if layer == 0:
            squares, first, rest = lax.optimization_barrier((squares, first, rest))
            own = first[:, 0]
            other = crossed(own, "c", 1)
            rest = jnp.concatenate([rest, crossed(rest, "zl", 2)], axis=0)
        if layer == layers - 1:
            squares, earlier = lax.optimization_barrier((squares, earlier))
        normed = values * lax.rsqrt(squares / total_channels + 1e-06)[:, None]
        stored = normed.astype(jnp.bfloat16)
        conv = jnp.zeros((row_count, values.shape[1]), jnp.float32)
        for k in range(n_taps):
            window = lax.dynamic_slice_in_dim(stored, REACH - offsets[layer, k], row_count, 0)
            conv = conv + coeffs[layer, k] * window.astype(jnp.float32)
        gated = (conv * jax.nn.silu(normed[REACH:])).astype(jnp.bfloat16)
        halves = [
            jnp.concatenate([gated[:, z * width + i * half : z * width + (i + 1) * half] for z in range(n_zh)], axis=1)
            for i in range(n_c)
        ]
        mine = jnp.where(c == 0, halves[0], halves[1])
        its = jnp.where(c == 0, halves[1], halves[0])
        partial = jnp.einsum("tk,xkn->xtn", mine, own, preferred_element_type=jnp.float32)
        partial = partial + jnp.einsum("tk,xkn->xtn", its, other, preferred_element_type=jnp.float32)
        partial = partial.astype(jnp.bfloat16)[entry_of]
        terms = lax.all_to_all(partial, "x", split_axis=0, concat_axis=0)
        mixed = jnp.sum(terms.astype(jnp.float32), axis=0)
        hidden = (hidden.astype(jnp.float32) + mixed).astype(jnp.bfloat16)
        if layer == 0:
            hidden, rest = lax.optimization_barrier((hidden, rest))
            rest = jnp.concatenate([rest, crossed(rest, "zl", 1)], axis=0)
        results.append(hidden)
    last = lax.ppermute(results[-1], TURNED, back)
    return jnp.concatenate([earlier, last[None]], axis=0)


def solution(mesh):
    fine = Mesh(mesh.devices.reshape(4, 8, 2, 4, 4), ("y", "zl", "c", "x", "zh"))
    dp = ("x", "zh")
    in_specs = (P(SECTION, dp), P(None, dp, None), P(None, None, dp), P())
    out_specs = P(None, SECTION, dp)
    return jax.shard_map(body, mesh=fine, in_specs=in_specs, out_specs=out_specs, check_vma=False)
```

```python
import jax
import jax.numpy as jnp
from jax import lax
from jax.sharding import Mesh, PartitionSpec as P

REACH = 64
SECTION = ("y", "zl", "c")
TURNED = ("y", "zl", "zh")
PLACE = ("zl", "c", "zh")


def turn_pairs(n_y, n_zl, n_zh):
    pairs = []
    for y in range(n_y):
        for zl in range(n_zl):
            for zh in range(n_zh):
                q, r = divmod(zl, 2)
                source = (y * n_zl + zl) * n_zh + zh
                target = ((zh + y) % n_y * n_zl + y + n_y * r) * n_zh + q
                pairs.append((source, target))
    return pairs


def halo_pairs(n_y, n_zl, n_c, n_zh):
    places = []
    for y in range(n_y):
        for zl in range(n_zl):
            for c in range(n_c):
                q, r = divmod(zl, 2)
                places.append(((y + n_y * r) * n_c + c) * n_zh + q)
    return list(zip(places[:-1], places[1:]))


def swap_pairs(n_y, n_zl, bit):
    pairs = []
    for y in range(n_y):
        for zl in range(n_zl):
            other = zl ^ bit
            pairs.append((y * n_zl + zl, (y + other - zl) % n_y * n_zl + other))
    return pairs


def split_rows(gated, rotation, c, n_zh, n_c):
    half = gated.shape[1] // (n_zh * n_c)
    choices = []
    for turn in range(n_zh):
        for i in range(n_c):
            starts = [((z + turn) % n_zh * n_c + i) * half for z in range(n_zh)]
            choices.append(jnp.concatenate([gated[:, start : start + half] for start in starts], axis=1))
    swapped = [choices[k ^ 1] for k in range(len(choices))]
    which = rotation * n_c + c
    return lax.select_n(which, *choices), lax.select_n(which, *swapped)


def after(value, *others):
    return lax.optimization_barrier((value, *others))[0]


def body(signal, mixing, taps, offsets):
    row_count, width = signal.shape
    layers, n_taps = taps.shape[:2]
    n_x, n_y, n_zl, n_c, n_zh = (lax.axis_size(a) for a in ("x", "y", "zl", "c", "zh"))
    y, zl, c = lax.axis_index("y"), lax.axis_index("zl"), lax.axis_index("c")
    total_channels = n_x * n_zh * width
    there = turn_pairs(n_y, n_zl, n_zh)
    back = [(target, source) for source, target in there]
    forward = halo_pairs(n_y, n_zl, n_c, n_zh)

    hidden = lax.ppermute(signal, TURNED, there)

    low_bits = zl % n_y
    block = (y - low_bits) % n_y
    half = width // n_c
    share = lax.dynamic_slice(mixing, (0, c * half, (low_bits * n_zh + block) * width), (layers, half, width))
    high = lax.reduce_precision(taps, 8, 7)
    low = (taps - high).astype(jnp.bfloat16)
    n_tap_rows = layers * n_taps
    sent = jnp.concatenate(
        [
            share.reshape(layers * half, width),
            high.astype(jnp.bfloat16).reshape(n_tap_rows, width),
            low.reshape(n_tap_rows, width),
            jnp.zeros((-2 * n_tap_rows % 16, width), jnp.bfloat16),
        ],
        axis=0,
    )
    got = lax.all_gather(sent, "zh", axis=0)
    hidden, got = lax.optimization_barrier((hidden, got))
    coeffs = got[:, layers * half :][(jnp.arange(n_zh) - low_bits) % n_zh].astype(jnp.float32)
    coeffs = coeffs[:, :n_tap_rows] + coeffs[:, n_tap_rows : 2 * n_tap_rows]
    coeffs = coeffs.transpose(1, 0, 2).reshape(layers, n_taps, n_zh * width)
    shares = got[:, : layers * half].reshape(n_zh, layers, half, width).transpose(1, 0, 2, 3)
    first = shares[:1].reshape(1, 1, n_zh * half, width)
    rest = shares[1:].reshape(1, layers - 1, n_zh * half, width)

    swap1, swap2 = swap_pairs(n_y, n_zl, 1), swap_pairs(n_y, n_zl, 2)
    first = jnp.concatenate([first, lax.ppermute(first, ("y", "zl"), swap2)], axis=0)
    order = jnp.array([0, 2, 1, 3])
    entry_of = order[jnp.arange(n_x) ^ low_bits]
    new_y = (lax.axis_index("zh") == 0) & (zl < n_y) & (c == 0)
    returned = []
    own = other = None
    for layer in range(layers):
        wide = lax.all_gather(hidden, "y", axis=1, tiled=True)
        if layer == 0:
            wide, first = lax.optimization_barrier((wide, first))
            first = jnp.concatenate([first, lax.ppermute(first, ("y", "zl"), swap1)], axis=0)
        else:
            own = rest[:, layer - 1]
            other = lax.ppermute(after(own, wide), "c", [(0, 1), (1, 0)])
        before = lax.ppermute(wide[row_count - REACH :], PLACE, forward)
        before = jnp.where(new_y, jnp.roll(before, width, axis=1), before)
        values = jnp.concatenate([before, wide], axis=0).astype(jnp.float32)
        squares = lax.psum(jnp.sum(values * values, axis=-1), "x")
        if layer == 0:
            squares, first, rest = lax.optimization_barrier((squares, first, rest))
            own = first[:, 0]
            other = lax.ppermute(own, "c", [(0, 1), (1, 0)])
            rest = jnp.concatenate([rest, lax.ppermute(rest, ("y", "zl"), swap2)], axis=0)
        normed = values * lax.rsqrt(squares / total_channels + 1e-06)[:, None]
        stored = normed.astype(jnp.bfloat16)
        conv = jnp.zeros((row_count, values.shape[1]), jnp.float32)
        for k in range(n_taps):
            window = lax.dynamic_slice_in_dim(stored, REACH - offsets[layer, k], row_count, 0)
            conv = conv + coeffs[layer, k] * window.astype(jnp.float32)
        gated = (conv * jax.nn.silu(normed[REACH:])).astype(jnp.bfloat16)
        mine, its = split_rows(gated, low_bits, c, n_zh, n_c)
        partial = jnp.einsum("tk,xkn->xtn", mine, own, preferred_element_type=jnp.float32)
        partial = partial + jnp.einsum("tk,xkn->xtn", its, other, preferred_element_type=jnp.float32)
        partial = partial.astype(jnp.bfloat16)[entry_of]
        if layer > 0:
            returned.append(lax.ppermute(hidden, TURNED, back))
            partial, returned[-1] = lax.optimization_barrier((partial, returned[-1]))
        terms = lax.all_to_all(partial, "x", split_axis=0, concat_axis=0)
        mixed = jnp.sum(terms.astype(jnp.float32), axis=0)
        hidden = (hidden.astype(jnp.float32) + mixed).astype(jnp.bfloat16)
        if layer == 0:
            hidden, rest = lax.optimization_barrier((hidden, rest))
            rest = jnp.concatenate([rest, lax.ppermute(rest, ("y", "zl"), swap1)], axis=0)
    returned.append(lax.ppermute(hidden, TURNED, back))
    return jnp.stack(returned)


def solution(mesh):
    fine = Mesh(mesh.devices.reshape(4, 8, 2, 4, 4), ("y", "zl", "c", "x", "zh"))
    dp = ("x", "zh")
    in_specs = (P(SECTION, dp), P(None, dp, None), P(None, None, dp), P())
    out_specs = P(None, SECTION, dp)
    return jax.shard_map(body, mesh=fine, in_specs=in_specs, out_specs=out_specs, check_vma=False)
```

```python
import jax
import jax.numpy as jnp
from jax import lax
from jax.sharding import Mesh, PartitionSpec as P

REACH = 64
SECTION = ("y", "zq", "zp", "c")
MOVED = ("zq", "zp", "zh")
PLACE = ("y", "zq", "c", "zh")


def moved_pairs(n_zl, n_zh):
    pairs = []
    for zl in range(n_zl):
        for zh in range(n_zh):
            pairs.append((zl * n_zh + zh, (zl % 2 * n_zh + zh) * n_zh + zl // 2))
    return pairs


def halo_pairs(n_y, n_zl, n_c, n_zh):
    places = []
    for y in range(n_y):
        for zl in range(n_zl):
            for c in range(n_c):
                places.append(((y * 2 + zl % 2) * n_c + c) * n_zh + zl // 2)
    return list(zip(places[:-1], places[1:]))


def rotated(value, axis, steps):
    count = lax.axis_size(axis)
    return lax.ppermute(value, axis, [(source, (source + steps) % count) for source in range(count)])


def body(signal, mixing, taps, offsets):
    row_count, width = signal.shape
    layers, n_taps = taps.shape[:2]
    n_x, n_y, n_c, n_zh = (lax.axis_size(a) for a in ("x", "y", "c", "zh"))
    n_zl = lax.axis_size(("zq", "zp"))
    y, zp, c = lax.axis_index("y"), lax.axis_index("zp"), lax.axis_index("c")
    total_channels = n_x * n_zh * width
    there = moved_pairs(n_zl, n_zh)
    back = [(target, source) for source, target in there]
    forward = halo_pairs(n_y, n_zl, n_c, n_zh)

    hidden = lax.ppermute(signal, MOVED, there)

    half = width // n_c
    share = lax.dynamic_slice(mixing, (0, c * half, (y * n_zh + zp) * width), (layers, half, width))
    high = lax.reduce_precision(taps, 8, 7)
    low = (taps - high).astype(jnp.bfloat16)
    n_tap_rows = layers * n_taps
    sent = jnp.concatenate(
        [
            share.reshape(layers * half, width),
            high.astype(jnp.bfloat16).reshape(n_tap_rows, width),
            low.reshape(n_tap_rows, width),
            jnp.zeros((-2 * n_tap_rows % 16, width), jnp.bfloat16),
        ],
        axis=0,
    )
    got = lax.all_gather(sent, "zh", axis=0)
    hidden, got = lax.optimization_barrier((hidden, got))
    coeffs = got[:, layers * half :].astype(jnp.float32)
    coeffs = coeffs[:, :n_tap_rows] + coeffs[:, n_tap_rows : 2 * n_tap_rows]
    coeffs = coeffs.transpose(1, 0, 2).reshape(layers, n_taps, n_zh * width)
    first = lax.all_gather(got[:, :half], "c", axis=1, tiled=True).reshape(n_zh * width, width)
    hidden, first = lax.optimization_barrier((hidden, first))
    first = jnp.stack([first] + [rotated(first, "y", k) for k in range(1, n_y)])
    rest = [got[:, layer * half : (layer + 1) * half] for layer in range(1, layers)]
    entry_of = (y - jnp.arange(n_x)) % n_y
    returned = []
    for layer in range(layers):
        wide = lax.all_gather(hidden, "zp", axis=1, tiled=True)
        before = lax.ppermute(wide[row_count - REACH :], PLACE, forward)
        values = jnp.concatenate([before, wide], axis=0).astype(jnp.float32)
        squares = lax.psum(jnp.sum(values * values, axis=-1), "x")
        if layer == 0:
            squares, rest = lax.optimization_barrier((squares, rest))
            rest = [lax.all_gather(part, "c", axis=1, tiled=True).reshape(n_zh * width, width) for part in rest]
            later = lax.all_gather(jnp.stack(rest), "y", axis=0)
        normed = values * lax.rsqrt(squares / total_channels + 1e-06)[:, None]
        stored = normed.astype(jnp.bfloat16)
        conv = jnp.zeros((row_count, values.shape[1]), jnp.float32)
        for k in range(n_taps):
            window = lax.dynamic_slice_in_dim(stored, REACH - offsets[layer, k], row_count, 0)
            conv = conv + coeffs[layer, k] * window.astype(jnp.float32)
        gated = (conv * jax.nn.silu(normed[REACH:])).astype(jnp.bfloat16)
        tile = first if layer == 0 else later[:, layer - 1]
        partial = jnp.einsum("tk,xkn->xtn", gated, tile, preferred_element_type=jnp.float32).astype(jnp.bfloat16)
        if layer == 0:
            partial = partial[entry_of]
        else:
            returned.append(lax.ppermute(hidden, MOVED, back))
            partial, returned[-1] = lax.optimization_barrier((partial, returned[-1]))
        terms = lax.all_to_all(partial, "x", split_axis=0, concat_axis=0)
        mixed = jnp.sum(terms.astype(jnp.float32), axis=0)
        hidden = (hidden.astype(jnp.float32) + mixed).astype(jnp.bfloat16)
    returned.append(lax.ppermute(hidden, MOVED, back))
    return jnp.stack(returned)


def solution(mesh):
    fine = Mesh(mesh.devices.reshape(4, 2, 4, 2, 4, 4), ("y", "zq", "zp", "c", "x", "zh"))
    dp = ("x", "zh")
    in_specs = (P(SECTION, dp), P(None, dp, None), P(None, None, dp), P())
    out_specs = P(None, SECTION, dp)
    return jax.shard_map(body, mesh=fine, in_specs=in_specs, out_specs=out_specs, check_vma=False)
```

```python
import jax
import jax.numpy as jnp
from jax import lax
from jax.sharding import Mesh, PartitionSpec as P

C = 4096
REACH = 64
SECTION = ("y", "zl", "c")
PLACE = ("y", "zl", "c", "zh")


def rotated(value, axis, steps):
    count = lax.axis_size(axis)
    return lax.ppermute(value, axis, [(source, (source + steps) % count) for source in range(count)])


def halo_pairs(n_y, n_zl, n_c, n_zh):
    n_section = n_y * n_zl * n_c
    pairs = []
    for section in range(n_section - 1):
        step = 1 if (section + 1) % (n_zl * n_c) == 0 else 0
        for zh in range(n_zh):
            pairs.append((section * n_zh + zh, (section + 1) * n_zh + (zh + step) % n_zh))
    return pairs


def crossed_weights(mixing):
    layers, depth, width = mixing.shape
    n_y, n_c, n_zh = lax.axis_size("y"), lax.axis_size("c"), lax.axis_size("zh")
    y, c, parity = lax.axis_index("y"), lax.axis_index("c"), lax.axis_index("zl") % 2
    columns = width // n_y
    rows = depth // n_c
    first = lax.dynamic_slice(mixing, (0, c * rows, y * columns), (1, rows, columns))
    first = first.reshape(rows, n_zh, columns // n_zh).transpose(1, 0, 2)
    few = rows // 2
    rest = lax.dynamic_slice(mixing, (1, c * rows + parity * few, y * columns), (layers - 1, few, columns))
    rest = rest.reshape(layers - 1, few, n_zh, columns // n_zh).transpose(2, 0, 1, 3)
    rest = rest.reshape(n_zh, (layers - 1) * few, columns // n_zh)
    got = lax.all_to_all(jnp.concatenate([first, rest], axis=1), "zh", split_axis=0, concat_axis=0)
    return got[:, :rows], got[:, rows:].reshape(n_zh, layers - 1, few, columns // n_zh)


def body(signal, mixing, taps, offsets):
    row_count, channel_count = signal.shape
    layers, n_taps = taps.shape[:2]
    n_y, n_zl, n_c, n_zh = (lax.axis_size(a) for a in ("y", "zl", "c", "zh"))
    forward = halo_pairs(n_y, n_zl, n_c, n_zh)
    first, rest = crossed_weights(mixing)
    signal, first, rest = lax.optimization_barrier((signal, first, rest))
    partner = lax.ppermute(rest, "zl", [(i, i ^ 1) for i in range(n_zl)])
    even = lax.axis_index("zl") % 2 == 0
    own = lax.all_gather(first, "c", axis=1, tiled=True).reshape(-1, channel_count)
    turned = jnp.stack([own] + [rotated(own, "y", k) for k in range(1, n_y)])
    high = lax.reduce_precision(taps, 8, 7)
    low = (taps - high).astype(jnp.bfloat16)
    tap_rows = jnp.concatenate(
        [high.astype(jnp.bfloat16).reshape(-1, channel_count), low.reshape(-1, channel_count)], axis=0
    )
    n_tap_rows = layers * n_taps
    tap_rows = jnp.pad(tap_rows, ((0, -2 * n_tap_rows % 16), (0, 0)))
    hidden = signal
    results = []
    for layer in range(layers):
        if layer == 0:
            wide = lax.all_gather(jnp.concatenate([hidden, tap_rows], axis=0), "zh", axis=1, tiled=True)
            coeffs = wide[row_count : row_count + 2 * n_tap_rows].astype(jnp.float32)
            coeffs = (coeffs[:n_tap_rows] + coeffs[n_tap_rows:]).reshape(layers, n_taps, -1)
            wide = wide[:row_count]
            wide, turned, partner = lax.optimization_barrier((wide, turned, partner))
            pair = jnp.stack([jnp.where(even, rest, partner), jnp.where(even, partner, rest)], axis=2)
            pair = pair.reshape(n_zh, layers - 1, -1, channel_count)
            whole = [lax.all_gather(pair[:, i], "c", axis=1, tiled=True) for i in range(layers - 1)]
            wide, whole = lax.optimization_barrier((wide, whole))
            whole = jnp.stack([part.reshape(-1, channel_count) for part in whole])
            later = lax.all_gather(whole, "y", axis=0)
        else:
            wide = lax.all_gather(hidden, "zh", axis=1, tiled=True)
        before = lax.ppermute(wide[row_count - REACH :], PLACE, forward)
        values = jnp.concatenate([before, wide], axis=0).astype(jnp.float32)
        squares = lax.psum(jnp.sum(values * values, axis=-1), "x")
        normed = values * lax.rsqrt(squares / C + 1e-06)[:, None]
        stored = normed.astype(jnp.bfloat16)
        conv = jnp.zeros((row_count, values.shape[1]), jnp.float32)
        for k in range(n_taps):
            window = lax.dynamic_slice_in_dim(stored, REACH - offsets[layer, k], row_count, 0)
            conv = conv + coeffs[layer, k] * window.astype(jnp.float32)
        gated = (conv * jax.nn.silu(normed[REACH:])).astype(jnp.bfloat16)
        tile = turned if layer == 0 else later[:, layer - 1]
        partial = jnp.einsum("tk,xkn->xtn", gated, tile, preferred_element_type=jnp.float32).astype(jnp.bfloat16)
        if layer == 0:
            partial = partial[(lax.axis_index("y") - jnp.arange(n_y)) % n_y]
        terms = lax.all_to_all(partial, "x", split_axis=0, concat_axis=0)
        mixed = jnp.sum(terms.astype(jnp.float32), axis=0)
        hidden = (hidden.astype(jnp.float32) + mixed).astype(jnp.bfloat16)
        results.append(hidden)
    return jnp.stack(results)


def solution(mesh):
    fine = Mesh(mesh.devices.reshape(4, 8, 2, 4, 4), ("y", "zl", "c", "x", "zh"))
    dp = ("x", "zh")
    in_specs = (P(SECTION, dp), P(None, dp, None), P(None, None, dp), P())
    out_specs = P(None, SECTION, dp)
    return jax.shard_map(body, mesh=fine, in_specs=in_specs, out_specs=out_specs, check_vma=False)
```

```python
import jax
import jax.numpy as jnp
from jax import lax
from jax.sharding import Mesh, PartitionSpec as P

REACH = 64
SECTION = ("y", "zq", "zp", "c")
MOVED = ("zq", "zp", "zh")
PLACE = ("y", "zq", "c", "zh")


def moved_pairs(n_zl, n_zh):
    pairs = []
    for zl in range(n_zl):
        for zh in range(n_zh):
            pairs.append((zl * n_zh + zh, (zl % 2 * n_zh + zh) * n_zh + zl // 2))
    return pairs


def halo_pairs(n_y, n_zl, n_c, n_zh):
    places = []
    for y in range(n_y):
        for zl in range(n_zl):
            for c in range(n_c):
                places.append(((y * 2 + zl % 2) * n_c + c) * n_zh + zl // 2)
    return list(zip(places[:-1], places[1:]))


def first_halo_pairs(n_y, n_zl, n_c, n_zh):
    n_zp = n_zl // 2
    pairs = []
    for section in range(n_y * n_zl * n_c - 1):
        zl, c = (section + 1) // n_c % n_zl, (section + 1) % n_c
        y = (section + 1) // (n_c * n_zl)
        for zh in range(n_zh):
            target = (((y * 2 + zl % 2) * n_zp + zh) * n_c + c) * n_zh + zl // 2
            pairs.append((section * n_zh + zh, target))
    return pairs


def rotated(value, axis, steps):
    count = lax.axis_size(axis)
    return lax.ppermute(value, axis, [(source, (source + steps) % count) for source in range(count)])


def body(signal, mixing, taps, offsets):
    row_count, width = signal.shape
    layers, n_taps = taps.shape[:2]
    n_x, n_y, n_c, n_zh = (lax.axis_size(a) for a in ("x", "y", "c", "zh"))
    n_zl = lax.axis_size(("zq", "zp"))
    y, zp, c = lax.axis_index("y"), lax.axis_index("zp"), lax.axis_index("c")
    total_channels = n_x * n_zh * width
    there = moved_pairs(n_zl, n_zh)
    back = [(target, source) for source, target in there]
    forward = halo_pairs(n_y, n_zl, n_c, n_zh)

    hidden = lax.ppermute(signal, MOVED, there)
    before = lax.ppermute(signal[row_count - REACH :], SECTION + ("zh",), first_halo_pairs(n_y, n_zl, n_c, n_zh))
    starts = (REACH - offsets).astype(jnp.uint32)

    half = width // n_c
    share = lax.dynamic_slice(mixing, (0, c * half, (y * n_zh + zp) * width), (layers, half, width))
    high = lax.reduce_precision(taps, 8, 7)
    low = (taps - high).astype(jnp.bfloat16)
    n_tap_rows = layers * n_taps
    sent = jnp.concatenate(
        [
            share.reshape(layers * half, width),
            high.astype(jnp.bfloat16).reshape(n_tap_rows, width),
            low.reshape(n_tap_rows, width),
            jnp.zeros((-2 * n_tap_rows % 16, width), jnp.bfloat16),
        ],
        axis=0,
    )
    got = lax.all_gather(sent, "zh", axis=0)
    hidden, before, got = lax.optimization_barrier((hidden, before, got))
    coeffs = got[:, layers * half :].astype(jnp.float32)
    coeffs = coeffs[:, :n_tap_rows] + coeffs[:, n_tap_rows : 2 * n_tap_rows]
    coeffs = coeffs.transpose(1, 0, 2).reshape(layers, n_taps, n_zh * width)
    whole = [
        lax.all_gather(got[:, layer * half : (layer + 1) * half], "c", axis=1, tiled=True).reshape(n_zh * width, width)
        for layer in range(layers)
    ]
    hidden, whole = lax.optimization_barrier((hidden, whole))
    turned = [whole[0]] + [rotated(whole[0], "y", k) for k in range(1, n_y)]
    rest = jnp.stack(whole[1:])
    entry_of = (y - jnp.arange(n_x)) % n_y
    returned = []
    for layer in range(layers):
        if layer > 0:
            before = lax.ppermute(hidden[row_count - REACH :], PLACE, forward)
        wide = lax.all_gather(jnp.concatenate([before, hidden], axis=0), "zp", axis=1, tiled=True)
        if layer == 0:
            wide, turned[1], turned[3], rest = lax.optimization_barrier((wide, turned[1], turned[3], rest))
            later = lax.all_gather(rest, "y", axis=0)
        values = wide.astype(jnp.float32)
        squares = lax.psum(jnp.sum(values * values, axis=-1), "x")
        if layer == 0:
            squares, turned[2] = lax.optimization_barrier((squares, turned[2]))
            first = jnp.stack(turned)
        normed = values * lax.rsqrt(squares / total_channels + 1e-06)[:, None]
        stored = normed.astype(jnp.bfloat16)
        conv = jnp.zeros((row_count, values.shape[1]), jnp.float32)
        for k in range(n_taps):
            window = lax.dynamic_slice(stored, (starts[layer, k], jnp.uint32(0)), (row_count, stored.shape[1]))
            conv = conv + coeffs[layer, k] * window.astype(jnp.float32)
        gated = (conv * jax.nn.silu(normed[REACH:])).astype(jnp.bfloat16)
        tile = first if layer == 0 else later[:, layer - 1]
        partial = jnp.einsum("tk,xkn->xtn", gated, tile, preferred_element_type=jnp.float32).astype(jnp.bfloat16)
        if layer == 0:
            partial = partial[entry_of]
        else:
            ready, _ = lax.optimization_barrier((hidden, before))
            partial, home = lax.optimization_barrier((partial, lax.ppermute(ready, MOVED, back)))
            returned.append(home)
        terms = lax.all_to_all(partial, "x", split_axis=0, concat_axis=0)
        mixed = jnp.sum(terms.astype(jnp.float32), axis=0)
        hidden = (hidden.astype(jnp.float32) + mixed).astype(jnp.bfloat16)
    returned.append(lax.ppermute(hidden, MOVED, back))
    return jnp.stack(returned)


def solution(mesh):
    fine = Mesh(mesh.devices.reshape(4, 2, 4, 2, 4, 4), ("y", "zq", "zp", "c", "x", "zh"))
    dp = ("x", "zh")
    in_specs = (P(SECTION, dp), P(None, dp, None), P(None, None, dp), P())
    out_specs = P(None, SECTION, dp)
    return jax.shard_map(body, mesh=fine, in_specs=in_specs, out_specs=out_specs, check_vma=False)
```

```python
import jax
import jax.numpy as jnp
from jax import lax
from jax.sharding import Mesh, PartitionSpec as P

REACH = 64
SECTION = ("y", "zq", "zp", "c")
MOVED = ("zq", "zp", "zh")
PLACE = ("y", "zq", "c", "zh")


def moved_pairs(n_zl, n_zh):
    pairs = []
    for zl in range(n_zl):
        for zh in range(n_zh):
            pairs.append((zl * n_zh + zh, (zl % 2 * n_zh + zh) * n_zh + zl // 2))
    return pairs


def halo_pairs(n_y, n_zl, n_c, n_zh):
    places = []
    for y in range(n_y):
        for zl in range(n_zl):
            for c in range(n_c):
                places.append(((y * 2 + zl % 2) * n_c + c) * n_zh + zl // 2)
    return list(zip(places[:-1], places[1:]))


def first_halo_pairs(n_y, n_zl, n_c, n_zh):
    n_zp = n_zl // 2
    pairs = []
    for section in range(n_y * n_zl * n_c - 1):
        zl, c = (section + 1) // n_c % n_zl, (section + 1) % n_c
        y = (section + 1) // (n_c * n_zl)
        for zh in range(n_zh):
            target = (((y * 2 + zl % 2) * n_zp + zh) * n_c + c) * n_zh + zl // 2
            pairs.append((section * n_zh + zh, target))
    return pairs


def rotated(value, axis, steps):
    count = lax.axis_size(axis)
    return lax.ppermute(value, axis, [(source, (source + steps) % count) for source in range(count)])


def body(signal, mixing, taps, offsets):
    row_count, width = signal.shape
    layers, n_taps = taps.shape[:2]
    n_x, n_y, n_c, n_zh = (lax.axis_size(a) for a in ("x", "y", "c", "zh"))
    n_zl = lax.axis_size(("zq", "zp"))
    y, zp, c = lax.axis_index("y"), lax.axis_index("zp"), lax.axis_index("c")
    total_channels = n_x * n_zh * width
    there = moved_pairs(n_zl, n_zh)
    back = [(target, source) for source, target in there]
    forward = halo_pairs(n_y, n_zl, n_c, n_zh)

    hidden = lax.ppermute(signal, MOVED, there)
    before = lax.ppermute(signal[row_count - REACH :], SECTION + ("zh",), first_halo_pairs(n_y, n_zl, n_c, n_zh))
    starts = (REACH - offsets).astype(jnp.uint32)

    half = width // n_c
    share = lax.dynamic_slice(mixing, (0, c * half, (y * n_zh + zp) * width), (layers, half, width))
    high = lax.reduce_precision(taps, 8, 7)
    low = (taps - high).astype(jnp.bfloat16)
    n_tap_rows = layers * n_taps
    sent = jnp.concatenate(
        [
            share.reshape(layers * half, width),
            high.astype(jnp.bfloat16).reshape(n_tap_rows, width),
            low.reshape(n_tap_rows, width),
            jnp.zeros((-2 * n_tap_rows % 16, width), jnp.bfloat16),
        ],
        axis=0,
    )
    got = lax.all_gather(sent, "zh", axis=0)
    hidden, before, got = lax.optimization_barrier((hidden, before, got))
    coeffs = got[:, layers * half :].astype(jnp.float32)
    coeffs = coeffs[:, :n_tap_rows] + coeffs[:, n_tap_rows : 2 * n_tap_rows]
    coeffs = coeffs.transpose(1, 0, 2).reshape(layers, n_taps, n_zh * width)
    whole = [
        lax.all_gather(got[:, layer * half : (layer + 1) * half], "c", axis=1, tiled=True).reshape(n_zh * width, width)
        for layer in range(layers)
    ]
    hidden, whole = lax.optimization_barrier((hidden, whole))
    turned = [whole[0]] + [rotated(whole[0], "y", k) for k in range(1, n_y)]
    rest = jnp.stack(whole[1:])
    entry_of = (y - jnp.arange(n_x)) % n_y
    returned = []
    for layer in range(layers):
        if layer > 0:
            before = lax.ppermute(hidden[row_count - REACH :], PLACE, forward)
        wide = lax.all_gather(jnp.concatenate([before, hidden], axis=0), "zp", axis=1, tiled=True)
        if layer == 0:
            wide, turned[1], turned[3], rest = lax.optimization_barrier((wide, turned[1], turned[3], rest))
            later = lax.all_gather(rest, "y", axis=0)
        values = wide.astype(jnp.float32)
        squares = lax.psum(jnp.sum(values * values, axis=-1), "x")
        if layer == 0:
            squares, turned[2] = lax.optimization_barrier((squares, turned[2]))
            first = jnp.stack(turned)
        normed = values * lax.rsqrt(squares / total_channels + 1e-06)[:, None]
        stored = lax.optimization_barrier(normed.astype(jnp.bfloat16))
        conv = jnp.zeros((row_count, values.shape[1]), jnp.float32)
        for k in range(n_taps):
            window = lax.dynamic_slice(stored, (starts[layer, k], jnp.uint32(0)), (row_count, stored.shape[1]))
            conv = conv + coeffs[layer, k] * window.astype(jnp.float32)
        gated = lax.optimization_barrier((conv * jax.nn.silu(normed[REACH:])).astype(jnp.bfloat16))
        tile = first if layer == 0 else later[:, layer - 1]
        partial = jnp.einsum("tk,xkn->xtn", gated, tile, preferred_element_type=jnp.float32).astype(jnp.bfloat16)
        if layer == 0:
            partial = partial[entry_of]
        else:
            ready, _ = lax.optimization_barrier((hidden, wide))
            partial, home = lax.optimization_barrier((partial, lax.ppermute(ready, MOVED, back)))
            returned.append(home)
        terms = lax.all_to_all(partial, "x", split_axis=0, concat_axis=0)
        mixed = jnp.sum(terms.astype(jnp.float32), axis=0)
        hidden = (hidden.astype(jnp.float32) + mixed).astype(jnp.bfloat16)
    returned.append(lax.ppermute(hidden, MOVED, back))
    return jnp.stack(returned)


def solution(mesh):
    fine = Mesh(mesh.devices.reshape(4, 2, 4, 2, 4, 4), ("y", "zq", "zp", "c", "x", "zh"))
    dp = ("x", "zh")
    in_specs = (P(SECTION, dp), P(None, dp, None), P(None, None, dp), P())
    out_specs = P(None, SECTION, dp)
    return jax.shard_map(body, mesh=fine, in_specs=in_specs, out_specs=out_specs, check_vma=False)
```

```python
import jax
import jax.numpy as jnp
from jax import lax
from jax.sharding import Mesh, PartitionSpec as P

REACH = 64
SECTION = ("y", "zq", "zp", "c")
MOVED = ("zq", "zp", "zh")
PLACE = ("y", "zq", "c", "zh")


def moved_pairs(n_zl, n_zh):
    pairs = []
    for zl in range(n_zl):
        for zh in range(n_zh):
            pairs.append((zl * n_zh + zh, (zl % 2 * n_zh + n_zh - 1 - zh) * n_zh + zl // 2))
    return pairs


def halo_pairs(n_y, n_zl, n_c, n_zh):
    places = []
    for y in range(n_y):
        for zl in range(n_zl):
            for c in range(n_c):
                places.append(((y * 2 + zl % 2) * n_c + c) * n_zh + zl // 2)
    return list(zip(places[:-1], places[1:]))


def first_halo_pairs(n_y, n_zl, n_c, n_zh):
    n_zp = n_zl // 2
    pairs = []
    for section in range(n_y * n_zl * n_c - 1):
        zl, c = (section + 1) // n_c % n_zl, (section + 1) % n_c
        y = (section + 1) // (n_c * n_zl)
        for zh in range(n_zh):
            target = (((y * 2 + zl % 2) * n_zp + n_zh - 1 - zh) * n_c + c) * n_zh + zl // 2
            pairs.append((section * n_zh + zh, target))
    return pairs


def rotated(value, axis, steps):
    count = lax.axis_size(axis)
    return lax.ppermute(value, axis, [(source, (source + steps) % count) for source in range(count)])


def body(signal, mixing, taps, offsets):
    row_count, width = signal.shape
    layers, n_taps = taps.shape[:2]
    n_x, n_y, n_c, n_zh = (lax.axis_size(a) for a in ("x", "y", "c", "zh"))
    n_zl = lax.axis_size(("zq", "zp"))
    y, zp, c = lax.axis_index("y"), lax.axis_index("zp"), lax.axis_index("c")
    total_channels = n_x * n_zh * width
    there = moved_pairs(n_zl, n_zh)
    back = [(target, source) for source, target in there]
    forward = halo_pairs(n_y, n_zl, n_c, n_zh)

    hidden = lax.ppermute(signal, MOVED, there)
    before = lax.ppermute(signal[row_count - REACH :], SECTION + ("zh",), first_halo_pairs(n_y, n_zl, n_c, n_zh))
    starts = REACH - offsets

    half = width // n_c
    share = lax.dynamic_slice(mixing, (0, c * half, (y * n_zh + n_zh - 1 - zp) * width), (layers, half, width))
    high = lax.reduce_precision(taps, 8, 7)
    low = (taps - high).astype(jnp.bfloat16)
    n_tap_rows = layers * n_taps
    sent = jnp.concatenate(
        [
            share.reshape(layers * half, width),
            high.astype(jnp.bfloat16).reshape(n_tap_rows, width),
            low.reshape(n_tap_rows, width),
            jnp.zeros((-2 * n_tap_rows % 16, width), jnp.bfloat16),
        ],
        axis=0,
    )
    got = lax.all_gather(sent, "zh", axis=0)
    hidden, before, got = lax.optimization_barrier((hidden, before, got))
    got = got[::-1]
    coeffs = got[:, layers * half :].astype(jnp.float32)
    coeffs = coeffs[:, :n_tap_rows] + coeffs[:, n_tap_rows : 2 * n_tap_rows]
    coeffs = coeffs.transpose(1, 0, 2).reshape(layers, n_taps, n_zh * width)
    whole = [
        lax.all_gather(got[:, layer * half : (layer + 1) * half], "c", axis=1, tiled=True).reshape(n_zh * width, width)
        for layer in range(layers)
    ]
    hidden, whole = lax.optimization_barrier((hidden, whole))
    turned = [whole[0]] + [rotated(whole[0], "y", k) for k in range(1, n_y)]
    rest = jnp.stack(whole[1:])
    entry_of = (y - jnp.arange(n_x)) % n_y
    returned = []
    for layer in range(layers):
        if layer > 0:
            before = lax.ppermute(hidden[row_count - REACH :], PLACE, forward)
        wide = lax.all_gather(jnp.concatenate([before, hidden], axis=0), "zp", axis=1, tiled=True)
        if layer == 0:
            wide, turned[1], turned[3], rest = lax.optimization_barrier((wide, turned[1], turned[3], rest))
            later = lax.all_gather(rest, "y", axis=0)
        values = wide.astype(jnp.float32)
        squares = lax.psum(jnp.sum(values * values, axis=-1), "x")
        if layer == 0:
            squares, turned[2] = lax.optimization_barrier((squares, turned[2]))
            first = jnp.stack(turned)
        normed = values * lax.rsqrt(squares / total_channels + 1e-06)[:, None]
        stored = lax.optimization_barrier(normed.astype(jnp.bfloat16))
        conv = jnp.zeros((row_count, values.shape[1]), jnp.float32)
        for k in range(n_taps):
            window = lax.dynamic_slice(
                stored, (starts[layer, k], 0), (row_count, stored.shape[1]), allow_negative_indices=False
            )
            conv = conv + coeffs[layer, k] * window.astype(jnp.float32)
        gated = lax.optimization_barrier((conv * jax.nn.silu(normed[REACH:])).astype(jnp.bfloat16))
        tile = first if layer == 0 else later[:, layer - 1]
        partial = jnp.einsum("tk,xkn->xtn", gated, tile, preferred_element_type=jnp.float32).astype(jnp.bfloat16)
        if layer == 0:
            partial = partial[entry_of]
        else:
            ready, _ = lax.optimization_barrier((hidden, wide))
            partial, home = lax.optimization_barrier((partial, lax.ppermute(ready, MOVED, back)))
            returned.append(home)
        terms = lax.all_to_all(partial, "x", split_axis=0, concat_axis=0)
        mixed = jnp.sum(terms.astype(jnp.float32), axis=0)
        hidden = (hidden.astype(jnp.float32) + mixed).astype(jnp.bfloat16)
    returned.append(lax.ppermute(hidden, MOVED, back))
    return jnp.stack(returned)


def solution(mesh):
    fine = Mesh(mesh.devices.reshape(4, 2, 4, 2, 4, 4), ("y", "zq", "zp", "c", "x", "zh"))
    dp = ("x", "zh")
    in_specs = (P(SECTION, dp), P(None, dp, None), P(None, None, dp), P())
    out_specs = P(None, SECTION, dp)
    return jax.shard_map(body, mesh=fine, in_specs=in_specs, out_specs=out_specs, check_vma=False)
```

```python
import jax
import jax.numpy as jnp
from jax import lax
from jax.sharding import Mesh, PartitionSpec as P

REACH = 64
SECTION = ("y", "zq", "zp", "c")
MOVED = ("zq", "zp", "zh")
PLACE = ("y", "zq", "c", "zh")


def moved_pairs(n_zl, n_zh):
    pairs = []
    for zl in range(n_zl):
        for zh in range(n_zh):
            pairs.append((zl * n_zh + zh, (zl % 2 * n_zh + n_zh - 1 - zh) * n_zh + zl // 2))
    return pairs


def halo_pairs(n_y, n_zl, n_c, n_zh):
    places = []
    for y in range(n_y):
        for zl in range(n_zl):
            for c in range(n_c):
                places.append(((y * 2 + zl % 2) * n_c + c) * n_zh + zl // 2)
    return list(zip(places[:-1], places[1:]))


def first_halo_pairs(n_y, n_zl, n_c, n_zh):
    n_zp = n_zl // 2
    pairs = []
    for section in range(n_y * n_zl * n_c - 1):
        zl, c = (section + 1) // n_c % n_zl, (section + 1) % n_c
        y = (section + 1) // (n_c * n_zl)
        for zh in range(n_zh):
            target = (((y * 2 + zl % 2) * n_zp + n_zh - 1 - zh) * n_c + c) * n_zh + zl // 2
            pairs.append((section * n_zh + zh, target))
    return pairs


def rotated(value, axis, steps):
    count = lax.axis_size(axis)
    return lax.ppermute(value, axis, [(source, (source + steps) % count) for source in range(count)])


def body(signal, mixing, taps, offsets):
    row_count, width = signal.shape
    layers, n_taps = taps.shape[:2]
    n_x, n_y, n_c, n_zh = (lax.axis_size(a) for a in ("x", "y", "c", "zh"))
    n_zl = lax.axis_size(("zq", "zp"))
    y, zp, c = lax.axis_index("y"), lax.axis_index("zp"), lax.axis_index("c")
    total_channels = n_x * n_zh * width
    there = moved_pairs(n_zl, n_zh)
    back = [(target, source) for source, target in there]
    forward = halo_pairs(n_y, n_zl, n_c, n_zh)

    starts = REACH - offsets

    half = width // n_c
    share = lax.dynamic_slice(mixing, (0, c * half, (y * n_zh + n_zh - 1 - zp) * width), (layers, half, width))
    high = lax.reduce_precision(taps, 8, 7)
    low = (taps - high).astype(jnp.bfloat16)
    n_tap_rows = layers * n_taps
    sent = jnp.concatenate(
        [
            share.reshape(layers * half, width),
            high.astype(jnp.bfloat16).reshape(n_tap_rows, width),
            low.reshape(n_tap_rows, width),
            jnp.zeros((-2 * n_tap_rows % 16, width), jnp.bfloat16),
        ],
        axis=0,
    )
    got = lax.all_gather(sent, "zh", axis=0)
    signal, got = lax.optimization_barrier((signal, got))
    hidden = lax.ppermute(signal, MOVED, there)
    before = lax.ppermute(signal[row_count - REACH :], SECTION + ("zh",), first_halo_pairs(n_y, n_zl, n_c, n_zh))
    got = got[::-1]
    coeffs = got[:, layers * half :].astype(jnp.float32)
    coeffs = coeffs[:, :n_tap_rows] + coeffs[:, n_tap_rows : 2 * n_tap_rows]
    coeffs = coeffs.transpose(1, 0, 2).reshape(layers, n_taps, n_zh * width)
    whole = [
        lax.all_gather(got[:, layer * half : (layer + 1) * half], "c", axis=1, tiled=True).reshape(n_zh * width, width)
        for layer in range(layers)
    ]
    hidden, before, whole = lax.optimization_barrier((hidden, before, whole))
    turned = [whole[0]] + [rotated(whole[0], "y", k) for k in range(1, n_y)]
    hidden, before, rest = lax.optimization_barrier((hidden, before, jnp.stack(whole[1:])))
    entry_of = (y - jnp.arange(n_x)) % n_y
    returned = []
    for layer in range(layers):
        if layer > 0:
            before = lax.ppermute(hidden[row_count - REACH :], PLACE, forward)
        wide = lax.all_gather(jnp.concatenate([before, hidden], axis=0), "zp", axis=1, tiled=True)
        if layer == 0:
            wide, turned[1], turned[3], rest = lax.optimization_barrier((wide, turned[1], turned[3], rest))
            later = lax.all_gather(rest, "y", axis=0)
        values = wide.astype(jnp.float32)
        squares = lax.psum(jnp.sum(values * values, axis=-1), "x")
        if layer == 0:
            squares, turned[2] = lax.optimization_barrier((squares, turned[2]))
            first = jnp.stack(turned)
        normed = values * lax.rsqrt(squares / total_channels + 1e-06)[:, None]
        stored, normed = lax.optimization_barrier((normed.astype(jnp.bfloat16), normed))
        conv = jnp.zeros((row_count, values.shape[1]), jnp.float32)
        for k in range(n_taps):
            window = lax.dynamic_slice(
                stored, (starts[layer, k], 0), (row_count, stored.shape[1]), allow_negative_indices=False
            )
            conv = conv + coeffs[layer, k] * window.astype(jnp.float32)
        gated = lax.optimization_barrier((conv * jax.nn.silu(normed[REACH:])).astype(jnp.bfloat16))
        tile = first if layer == 0 else later[:, layer - 1]
        partial = jnp.einsum("tk,xkn->xtn", gated, tile, preferred_element_type=jnp.float32).astype(jnp.bfloat16)
        if layer == 0:
            partial = partial[entry_of]
        else:
            ready, _ = lax.optimization_barrier((hidden, wide))
            partial, home = lax.optimization_barrier((partial, lax.ppermute(ready, MOVED, back)))
            returned.append(home)
        terms = lax.all_to_all(partial, "x", split_axis=0, concat_axis=0)
        mixed = jnp.sum(terms.astype(jnp.float32), axis=0)
        hidden = (hidden.astype(jnp.float32) + mixed).astype(jnp.bfloat16)
    returned.append(lax.ppermute(hidden, MOVED, back))
    return jnp.stack(returned)


def solution(mesh):
    fine = Mesh(mesh.devices.reshape(4, 2, 4, 2, 4, 4), ("y", "zq", "zp", "c", "x", "zh"))
    dp = ("x", "zh")
    in_specs = (P(SECTION, dp), P(None, dp, None), P(None, None, dp), P())
    out_specs = P(None, SECTION, dp)
    return jax.shard_map(body, mesh=fine, in_specs=in_specs, out_specs=out_specs, check_vma=False)
```

```python
import jax
import jax.numpy as jnp
from jax import lax
from jax.sharding import Mesh, PartitionSpec as P

REACH = 64
SECTION = ("y", "zq", "zp", "c")
MOVED = ("zq", "zp", "zh")
PLACE = ("y", "zq", "c", "zh")


def moved_pairs(n_zl, n_zh):
    pairs = []
    for zl in range(n_zl):
        for zh in range(n_zh):
            pairs.append((zl * n_zh + zh, (zl % 2 * n_zh + n_zh - 1 - zh) * n_zh + zl // 2))
    return pairs


def halo_pairs(n_y, n_zl, n_c, n_zh):
    places = []
    for y in range(n_y):
        for zl in range(n_zl):
            for c in range(n_c):
                places.append(((y * 2 + zl % 2) * n_c + c) * n_zh + zl // 2)
    return list(zip(places[:-1], places[1:]))


def first_halo_pairs(n_y, n_zl, n_c, n_zh):
    n_zp = n_zl // 2
    pairs = []
    for section in range(n_y * n_zl * n_c - 1):
        zl, c = (section + 1) // n_c % n_zl, (section + 1) % n_c
        y = (section + 1) // (n_c * n_zl)
        for zh in range(n_zh):
            target = (((y * 2 + zl % 2) * n_zp + n_zh - 1 - zh) * n_c + c) * n_zh + zl // 2
            pairs.append((section * n_zh + zh, target))
    return pairs


def rotated(value, axis, steps):
    count = lax.axis_size(axis)
    return lax.ppermute(value, axis, [(source, (source + steps) % count) for source in range(count)])


def body(signal, mixing, taps, offsets):
    row_count, width = signal.shape
    layers, n_taps = taps.shape[:2]
    n_x, n_y, n_c, n_zh = (lax.axis_size(a) for a in ("x", "y", "c", "zh"))
    n_zl = lax.axis_size(("zq", "zp"))
    y, zp, c = lax.axis_index("y"), lax.axis_index("zp"), lax.axis_index("c")
    total_channels = n_x * n_zh * width
    there = moved_pairs(n_zl, n_zh)
    back = [(target, source) for source, target in there]
    forward = halo_pairs(n_y, n_zl, n_c, n_zh)

    backs = lax.optimization_barrier([[offsets[layer, k] for k in range(n_taps)] for layer in range(layers)])
    starts = [[REACH - steps for steps in backs_of_layer] for backs_of_layer in backs]

    half = width // n_c
    share = lax.dynamic_slice(mixing, (0, c * half, (y * n_zh + n_zh - 1 - zp) * width), (layers, half, width))
    high = lax.reduce_precision(taps, 8, 7)
    low = (taps - high).astype(jnp.bfloat16)
    n_tap_rows = layers * n_taps
    sent = jnp.concatenate(
        [
            share.reshape(layers * half, width),
            high.astype(jnp.bfloat16).reshape(n_tap_rows, width),
            low.reshape(n_tap_rows, width),
            jnp.zeros((-2 * n_tap_rows % 16, width), jnp.bfloat16),
        ],
        axis=0,
    )
    got = lax.all_gather(sent, "zh", axis=0)
    signal, got = lax.optimization_barrier((signal, got))
    hidden = lax.ppermute(signal, MOVED, there)
    before = lax.ppermute(signal[row_count - REACH :], SECTION + ("zh",), first_halo_pairs(n_y, n_zl, n_c, n_zh))
    got = got[::-1]
    coeffs = got[:, layers * half :].astype(jnp.float32)
    coeffs = coeffs[:, :n_tap_rows] + coeffs[:, n_tap_rows : 2 * n_tap_rows]
    coeffs = coeffs.transpose(1, 0, 2).reshape(layers, n_taps, n_zh * width)
    whole = [
        lax.all_gather(got[:, layer * half : (layer + 1) * half], "c", axis=1, tiled=True).reshape(n_zh * width, width)
        for layer in range(layers)
    ]
    hidden, before, whole = lax.optimization_barrier((hidden, before, whole))
    turned = [whole[0]] + [rotated(whole[0], "y", k) for k in range(1, n_y)]
    hidden, before, rest = lax.optimization_barrier((hidden, before, jnp.stack(whole[1:])))
    entry_of = (y - jnp.arange(n_x)) % n_y
    returned = []
    for layer in range(layers):
        if layer > 0:
            before = lax.ppermute(hidden[row_count - REACH :], PLACE, forward)
        wide = lax.all_gather(jnp.concatenate([before, hidden], axis=0), "zp", axis=1, tiled=True)
        if layer == 0:
            wide, turned[1], turned[3], rest = lax.optimization_barrier((wide, turned[1], turned[3], rest))
            later = lax.all_gather(rest, "y", axis=0)
        values = wide.astype(jnp.float32)
        squares = lax.psum(jnp.sum(values * values, axis=-1), "x")
        if layer == 0:
            squares, turned[2] = lax.optimization_barrier((squares, turned[2]))
            first = jnp.stack(turned)
        normed = values * lax.rsqrt(squares / total_channels + 1e-06)[:, None]
        stored, normed = lax.optimization_barrier((normed.astype(jnp.bfloat16), normed))
        conv = jnp.zeros((row_count, values.shape[1]), jnp.float32)
        for k in range(n_taps):
            window = lax.dynamic_slice(
                stored, (starts[layer][k], 0), (row_count, stored.shape[1]), allow_negative_indices=False
            )
            conv = conv + coeffs[layer, k] * window.astype(jnp.float32)
        gated = lax.optimization_barrier((conv * jax.nn.silu(normed[REACH:])).astype(jnp.bfloat16))
        tile = first if layer == 0 else later[:, layer - 1]
        partial = jnp.einsum("tk,xkn->xtn", gated, tile, preferred_element_type=jnp.float32).astype(jnp.bfloat16)
        if layer == 0:
            partial = partial[entry_of]
        else:
            ready, _ = lax.optimization_barrier((hidden, wide))
            partial, home = lax.optimization_barrier((partial, lax.ppermute(ready, MOVED, back)))
            returned.append(home)
        terms = lax.all_to_all(partial, "x", split_axis=0, concat_axis=0)
        mixed = jnp.sum(terms.astype(jnp.float32), axis=0)
        hidden = (hidden.astype(jnp.float32) + mixed).astype(jnp.bfloat16)
    returned.append(lax.ppermute(hidden, MOVED, back))
    return jnp.stack(returned)


def solution(mesh):
    fine = Mesh(mesh.devices.reshape(4, 2, 4, 2, 4, 4), ("y", "zq", "zp", "c", "x", "zh"))
    dp = ("x", "zh")
    in_specs = (P(SECTION, dp), P(None, dp, None), P(None, None, dp), P())
    out_specs = P(None, SECTION, dp)
    return jax.shard_map(body, mesh=fine, in_specs=in_specs, out_specs=out_specs, check_vma=False)
```

```python
import jax
import jax.numpy as jnp
from jax import lax
from jax.sharding import Mesh, PartitionSpec as P

REACH = 64
SECTION = ("y", "zq", "zp", "c")
MOVED = ("zq", "zp", "zh")
PLACE = ("y", "zq", "c", "zh")


def moved_pairs(n_zl, n_zh):
    pairs = []
    for zl in range(n_zl):
        for zh in range(n_zh):
            pairs.append((zl * n_zh + zh, (zl % 2 * n_zh + n_zh - 1 - zh) * n_zh + zl // 2))
    return pairs


def halo_pairs(n_y, n_zl, n_c, n_zh):
    places = []
    for y in range(n_y):
        for zl in range(n_zl):
            for c in range(n_c):
                places.append(((y * 2 + zl % 2) * n_c + c) * n_zh + zl // 2)
    return list(zip(places[:-1], places[1:]))


def first_halo_pairs(n_y, n_zl, n_c, n_zh):
    n_zp = n_zl // 2
    pairs = []
    for section in range(n_y * n_zl * n_c - 1):
        zl, c = (section + 1) // n_c % n_zl, (section + 1) % n_c
        y = (section + 1) // (n_c * n_zl)
        for zh in range(n_zh):
            target = (((y * 2 + zl % 2) * n_zp + n_zh - 1 - zh) * n_c + c) * n_zh + zl // 2
            pairs.append((section * n_zh + zh, target))
    return pairs


def rotated(value, axis, steps):
    count = lax.axis_size(axis)
    return lax.ppermute(value, axis, [(source, (source + steps) % count) for source in range(count)])


def body(signal, mixing, taps, offsets):
    row_count, width = signal.shape
    layers, n_taps = taps.shape[:2]
    n_x, n_y, n_c, n_zh = (lax.axis_size(a) for a in ("x", "y", "c", "zh"))
    n_zl = lax.axis_size(("zq", "zp"))
    y, zp, c = lax.axis_index("y"), lax.axis_index("zp"), lax.axis_index("c")
    total_channels = n_x * n_zh * width
    there = moved_pairs(n_zl, n_zh)
    back = [(target, source) for source, target in there]
    forward = halo_pairs(n_y, n_zl, n_c, n_zh)

    backs = lax.optimization_barrier([[offsets[layer, k] for k in range(n_taps)] for layer in range(layers)])
    starts = [[REACH - steps for steps in backs_of_layer] for backs_of_layer in backs]

    half = width // n_c
    share = lax.dynamic_slice(mixing, (0, c * half, (y * n_zh + n_zh - 1 - zp) * width), (layers, half, width))
    high = lax.reduce_precision(taps, 8, 7)
    low = (taps - high).astype(jnp.bfloat16)
    n_tap_rows = layers * n_taps
    sent = jnp.concatenate(
        [
            share.reshape(layers * half, width),
            high.astype(jnp.bfloat16).reshape(n_tap_rows, width),
            low.reshape(n_tap_rows, width),
            jnp.zeros((-2 * n_tap_rows % 16, width), jnp.bfloat16),
        ],
        axis=0,
    )
    before = lax.ppermute(signal[row_count - REACH :], SECTION + ("zh",), first_halo_pairs(n_y, n_zl, n_c, n_zh))
    got = lax.all_gather(sent, "zh", axis=0)
    signal, before, got = lax.optimization_barrier((signal, before, got))
    hidden = lax.ppermute(signal, MOVED, there)
    got = got[::-1]
    coeffs = got[:, layers * half :].astype(jnp.float32)
    coeffs = coeffs[:, :n_tap_rows] + coeffs[:, n_tap_rows : 2 * n_tap_rows]
    coeffs = coeffs.transpose(1, 0, 2).reshape(layers, n_taps, n_zh * width)
    whole = [
        lax.all_gather(got[:, layer * half : (layer + 1) * half], "c", axis=1, tiled=True).reshape(n_zh * width, width)
        for layer in range(layers)
    ]
    hidden, before, whole = lax.optimization_barrier((hidden, before, whole))
    turned = [whole[0]] + [rotated(whole[0], "y", k) for k in range(1, n_y)]
    hidden, before, rest = lax.optimization_barrier((hidden, before, jnp.stack(whole[1:])))
    entry_of = (y - jnp.arange(n_x)) % n_y
    returned = []
    for layer in range(layers):
        if layer > 0:
            before = lax.ppermute(hidden[row_count - REACH :], PLACE, forward)
        wide = lax.all_gather(jnp.concatenate([before, hidden], axis=0), "zp", axis=1, tiled=True)
        if layer == 0:
            wide, turned[1], turned[3], rest = lax.optimization_barrier((wide, turned[1], turned[3], rest))
            later = lax.all_gather(rest, "y", axis=0)
        values = wide.astype(jnp.float32)
        squares = lax.psum(jnp.sum(values * values, axis=-1), "x")
        if layer == 0:
            squares, turned[2] = lax.optimization_barrier((squares, turned[2]))
            first = jnp.stack(turned)
        normed = values * lax.rsqrt(squares / total_channels + 1e-06)[:, None]
        stored, normed = lax.optimization_barrier((normed.astype(jnp.bfloat16), normed))
        conv = jnp.zeros((row_count, values.shape[1]), jnp.float32)
        for k in range(n_taps):
            window = lax.dynamic_slice(
                stored, (starts[layer][k], 0), (row_count, stored.shape[1]), allow_negative_indices=False
            )
            conv = conv + coeffs[layer, k] * window.astype(jnp.float32)
        gated = lax.optimization_barrier((conv * jax.nn.silu(normed[REACH:])).astype(jnp.bfloat16))
        tile = first if layer == 0 else later[:, layer - 1]
        partial = jnp.einsum("tk,xkn->xtn", gated, tile, preferred_element_type=jnp.float32).astype(jnp.bfloat16)
        if layer == 0:
            partial = partial[entry_of]
        else:
            ready, _ = lax.optimization_barrier((hidden, wide))
            partial, home = lax.optimization_barrier((partial, lax.ppermute(ready, MOVED, back)))
            returned.append(home)
        terms = lax.all_to_all(partial, "x", split_axis=0, concat_axis=0)
        mixed = jnp.sum(terms.astype(jnp.float32), axis=0)
        hidden = (hidden.astype(jnp.float32) + mixed).astype(jnp.bfloat16)
    returned.append(lax.ppermute(hidden, MOVED, back))
    return jnp.stack(returned)


def solution(mesh):
    fine = Mesh(mesh.devices.reshape(4, 2, 4, 2, 4, 4), ("y", "zq", "zp", "c", "x", "zh"))
    dp = ("x", "zh")
    in_specs = (P(SECTION, dp), P(None, dp, None), P(None, None, dp), P())
    out_specs = P(None, SECTION, dp)
    return jax.shard_map(body, mesh=fine, in_specs=in_specs, out_specs=out_specs, check_vma=False)
```
